32 devices in a mesh: mem: 2 (over x), gx: 4 (over y, core), gy: 4 (over z).
Axes of the slice: x: 2, y: 2, z: 4, core: 2. Of those that a mesh axis runs over, the one named last changes fastest.
Arguments:
- field: bfloat16 [2, 512, 512, 128], P('mem', 'gx', 'gy'), may hold values from -6 to 6
- spectral: bfloat16 [3, 32, 2, 32, 128, 128], P(None, ('gx', 'gy'), None, None, 'mem'), may hold values from -0.0546875 to 0.0546875
- pointwise: bfloat16 [3, 128, 128], replicated, may hold values from -0.5 to 0.5
- bias: float32 [3, 128], replicated, may hold values from -3 to 3
Outputs:
- field_out: bfloat16 [2, 512, 512, 128], P('mem', 'gx', 'gy')
The draws below stay inside these ranges and needn't reach their ends.
All inputs are finite; a program needn't handle non-finite values.
Results may differ from the reference program's by a relative error of at most 0.02.
Values may be sent and summed in bfloat16 or wider, within the bound.
A program may use at most 128 MiB of HBM per device.

```python
import math
import jax
import jax.numpy as jnp
from jax import lax

C = 128
KX = 32
KY = 32
NX = 512
NY = 512
LAYERS = 3
MEMBERS = 2
CXD = 128
N_GX = 4


def level_of(key, extent, cuts, least, largest):
    loudness, own = 1.0, jax.random.fold_in(key, 6)
    for axis_at, blocks in cuts:
        draws = jnp.exp(jax.random.uniform(jax.random.fold_in(own, axis_at), (blocks,), jnp.float32, least / len(cuts), largest / len(cuts)))
        loudness = loudness * jnp.repeat(draws, extent[axis_at] // blocks).reshape([-1 if axis == axis_at else 1 for axis in range(len(extent))])
    return loudness


def centred(stream_key, extent, scale, most, pieces=(), kind=jnp.bfloat16):
    array = jax.random.normal(stream_key, extent, jnp.float32) * scale
    if len(pieces) > 0:
        array = level_of(stream_key, extent, pieces, -0.22, 0.18) * array
    return jnp.clip(array, min=-most, max=most).astype(kind)


def setup_inputs(seed: int = 0) -> dict:
    streams_of = jax.random.split(jax.random.key(seed), 5)
    field = centred(streams_of[0], (MEMBERS, NX, NY, C), 1.0, 6.0, ((0, 2), (1, 4), (2, 4)))
    spectral = centred(streams_of[1], (LAYERS, KX, 2, KY, C, C), (100 * C) ** -0.5, 0.0546875, ((1, 16), (4, 2)))
    pointwise = centred(streams_of[2], (LAYERS, C, C), C ** -0.5, 0.5)
    bias = centred(streams_of[3], (LAYERS, C), 0.5, 3.0, (), jnp.float32)
    return {"field": field, "spectral": spectral, "pointwise": pointwise, "bias": bias}


def phase_angles(frequency, position, period):
    product = frequency[:, None] * position[None, :] % period
    return 2.0 * math.pi / period * product.astype(jnp.float32)

def x_frequencies():
    index = jnp.arange(KX, dtype=jnp.int32)
    return jnp.where(index < KX // 2, index, NX - KX + index)

def mode_product(coeffs, weights):
    coeffs = coeffs.astype(jnp.float32)
    weights = weights.astype(jnp.float32)
    real_part = jnp.einsum('kqi,kqio->kqo', coeffs[:, 0], weights[:, 0]) - jnp.einsum('kqi,kqio->kqo', coeffs[:, 1], weights[:, 1])
    imag_part = jnp.einsum('kqi,kqio->kqo', coeffs[:, 0], weights[:, 1]) + jnp.einsum('kqi,kqio->kqo', coeffs[:, 1], weights[:, 0])
    return jnp.stack([real_part, imag_part], axis=1)

def reference(field, spectral, pointwise, bias):
    positions_x = jnp.arange(NX, dtype=jnp.int32)
    positions_y = jnp.arange(NY, dtype=jnp.int32)
    angles_x = phase_angles(x_frequencies(), positions_x, NX)
    cosine_x = jnp.cos(angles_x).astype(jnp.bfloat16)
    sine_x = jnp.sin(angles_x).astype(jnp.bfloat16)
    forward_x = jnp.concatenate([cosine_x, -sine_x], axis=0)
    inverse_x = forward_x.T
    banded_x = forward_x.reshape(2 * KX, N_GX, CXD).astype(jnp.float32)
    angles_y = phase_angles(jnp.arange(KY, dtype=jnp.int32), positions_y, NY)
    cosine_y = jnp.cos(angles_y).T.astype(jnp.bfloat16)
    sine_y = jnp.sin(angles_y).T.astype(jnp.bfloat16)
    forward_y = jnp.concatenate([jnp.concatenate([cosine_y, -sine_y], axis=1), jnp.concatenate([sine_y, cosine_y], axis=1)], axis=0)
    doubling = jnp.where(jnp.arange(KY) == 0, 1.0, 2.0).astype(jnp.float32)[:, None]
    wcos = doubling * jnp.cos(angles_y)
    wsin = doubling * jnp.sin(angles_y)
    inverse_y = jnp.concatenate([jnp.concatenate([wcos, wsin], axis=1), jnp.concatenate([-wsin, wcos], axis=1)], axis=0).astype(jnp.bfloat16)
    scale_fwd = 1.0 / math.sqrt(NX * NY)
    scale_inv = 1.0 / math.sqrt(2 * KX * KY)

    def member_step(state):
        for level in range(LAYERS):
            bands = state.reshape(N_GX, CXD, NY, C).astype(jnp.float32)
            partial_x = jnp.einsum('kbx,bxyc->bkyc', banded_x, bands).astype(jnp.bfloat16)
            joined = jnp.concatenate([partial_x[:, :KX], partial_x[:, KX:]], axis=2)
            modes = jnp.einsum('bkyc,yq->kqc', joined.astype(jnp.float32), forward_y.astype(jnp.float32)) * scale_fwd
            modes = modes.reshape(KX, 2, KY, C).astype(jnp.bfloat16)
            mixed_modes = mode_product(modes, spectral[level]).astype(jnp.bfloat16)
            qmix = jnp.einsum('kqc,qy->kyc', mixed_modes.reshape(KX, 2 * KY, C).astype(jnp.float32), inverse_y.astype(jnp.float32)).astype(jnp.bfloat16)
            stacked = jnp.concatenate([qmix[:, :NY], qmix[:, NY:]], axis=0)
            spatial = jnp.einsum('xk,kyc->xyc', inverse_x.astype(jnp.float32), stacked.astype(jnp.float32))
            linear = jnp.dot(state.reshape(NX * NY, C), pointwise[level], preferred_element_type=jnp.float32).reshape(NX, NY, C)
            mixed = spatial * scale_inv + linear + bias[level].astype(jnp.float32)
            state = jax.nn.gelu(mixed, approximate=False).astype(jnp.bfloat16)
        return state
    return lax.map(member_step, field)
```

```python
import functools
import math

import jax
import jax.numpy as jnp
from jax import lax
from jax.experimental import pallas as pl
from jax.experimental.pallas import tpu as pltpu
from jax.sharding import PartitionSpec as P

KX = 32
KY = 32
NX = 512
NY = 512
LAYERS = 3
MESH = pl.DeviceIdType.MESH


def phase_angles(frequency, position, period):
    product = frequency[:, None] * position[None, :] % period
    return 2.0 * math.pi / period * product.astype(jnp.float32)


def exchange(mem, n_gx, n_gy, shape, level, pieces_ref, weights_ref, out_ref, got, held, sums,
             partial, arrived, send_a, recv_a, send_b, recv_b, send_c, recv_c, load_sem, own_sem):
    rows_j, depth = shape
    grid = n_gx * n_gy
    total = mem * grid
    m = lax.axis_index("mem")
    g = lax.axis_index("gx") * n_gy + lax.axis_index("gy")
    me = m * grid + g

    def place(mm, gg):
        return (mm, gg // n_gy, gg % n_gy)

    def place_all(d):
        return place(d // grid, d % grid)

    load = pltpu.make_async_copy(weights_ref.at[level], held, load_sem)
    load.start()
    barrier = pltpu.get_barrier_semaphore()

    def greet(k, c):
        pl.semaphore_signal(
            barrier, inc=1, device_id=place_all((me + k) % total), device_id_type=MESH
        )
        return c

    lax.fori_loop(1, total, greet, 0)
    pl.semaphore_wait(barrier, total - 1)

    def copy_a(k, dst, slot):
        return pltpu.make_async_remote_copy(
            src_ref=pieces_ref.at[dst],
            dst_ref=got.at[slot],
            send_sem=send_a.at[k],
            recv_sem=recv_a.at[k],
            device_id=place_all(dst),
            device_id_type=MESH,
        )

    def start_a(k, c):
        copy_a(k, (me + k) % total, me).start()
        return c

    lax.fori_loop(1, total, start_a, 0)
    own = pltpu.make_async_copy(pieces_ref.at[me], got.at[me], own_sem)
    own.start()
    own.wait()

    def wait_a(k, c):
        copy_a(k, (me + k) % total, (me + total - k) % total).wait()
        return c

    lax.fori_loop(1, total, wait_a, 0)
    items = rows_j * depth
    for mm in range(mem):
        acc = got[mm * grid].astype(jnp.float32)
        for gg in range(1, grid):
            acc = acc + got[mm * grid + gg].astype(jnp.float32)
        sums[mm] = acc[:items]
        sums[mem + mm] = acc[items:]
    load.wait()
    lanes = sums.shape[-1]
    wide = lanes // mem
    lane = lax.broadcasted_iota(jnp.int32, (2 * mem, lanes), 1)

    def mix(b, c):
        j = b // depth
        qq = b % depth
        x = sums[:, pl.ds(b, 1), :].reshape(2 * mem, lanes)
        parts = [
            jnp.where((lane >= h * wide) & (lane < (h + 1) * wide), x, 0.0) for h in range(mem)
        ]
        x = jnp.concatenate(parts, axis=0).astype(jnp.bfloat16)
        by_re = jnp.dot(x, held[j, 0, qq], preferred_element_type=jnp.float32)
        by_im = jnp.dot(x, held[j, 1, qq], preferred_element_type=jnp.float32)
        for h in range(mem):
            lo = h * 2 * mem
            re = by_re[lo : lo + mem] - by_im[lo + mem : lo + 2 * mem]
            im = by_im[lo : lo + mem] + by_re[lo + mem : lo + 2 * mem]
            for mm in range(mem):
                partial[mm, h, pl.ds(b, 1), :] = re[mm : mm + 1]
                partial[mm, mem + h, pl.ds(b, 1), :] = im[mm : mm + 1]
        return c

    lax.fori_loop(0, items, mix, 0, unroll=4)

    def copy_b(k, dst, slot):
        return pltpu.make_async_remote_copy(
            src_ref=partial.at[dst],
            dst_ref=arrived.at[slot],
            send_sem=send_b.at[k],
            recv_sem=recv_b.at[k],
            device_id=place(dst, g),
            device_id_type=MESH,
        )

    def start_b(k, c):
        copy_b(k, (m + k) % mem, k).start()
        return c

    lax.fori_loop(1, mem, start_b, 0)

    def wait_b(k, c):
        copy_b(k, (m + k) % mem, k).wait()
        return c

    lax.fori_loop(1, mem, wait_b, 0)
    block = partial[m]
    for k in range(1, mem):
        block = block + arrived[k]
    out_ref[g] = block.astype(out_ref.dtype)

    def copy_c(k, slot):
        return pltpu.make_async_remote_copy(
            src_ref=out_ref.at[g],
            dst_ref=out_ref.at[slot],
            send_sem=send_c.at[k],
            recv_sem=recv_c.at[k],
            device_id=place(m, (g + k) % grid),
            device_id_type=MESH,
        )

    def start_c(k, c):
        copy_c(k, g).start()
        return c

    lax.fori_loop(1, grid, start_c, 0)

    def wait_c(k, c):
        copy_c(k, (g + grid - k) % grid).wait()
        return c

    lax.fori_loop(1, grid, wait_c, 0)


def spectral_mix(pieces, weights, level, own_rows, depth):
    mem = lax.axis_size("mem")
    n_gx = lax.axis_size("gx")
    n_gy = lax.axis_size("gy")
    grid = n_gx * n_gy
    total = mem * grid
    channels = pieces.shape[-1]
    items = own_rows * depth
    dma = pltpu.SemaphoreType.DMA
    return pl.pallas_call(
        functools.partial(exchange, mem, n_gx, n_gy, (own_rows, depth), level),
        out_shape=jax.ShapeDtypeStruct((grid, 2 * mem, items, channels), jnp.bfloat16),
        in_specs=[
            pl.BlockSpec(memory_space=pltpu.VMEM),
            pl.BlockSpec(memory_space=pl.ANY),
        ],
        out_specs=pl.BlockSpec(memory_space=pltpu.VMEM),
        scratch_shapes=[
            pltpu.VMEM(pieces.shape, jnp.bfloat16),
            pltpu.VMEM(weights.shape[1:], jnp.bfloat16),
            pltpu.VMEM((2 * mem, items, channels), jnp.float32),
            pltpu.VMEM((mem, 2 * mem, items, channels), jnp.float32),
            pltpu.VMEM((mem, 2 * mem, items, channels), jnp.float32),
            dma((total,)),
            dma((total,)),
            dma((mem,)),
            dma((mem,)),
            dma((grid,)),
            dma((grid,)),
            dma,
            dma,
        ],
        compiler_params=pltpu.CompilerParams(
            collective_id=level, has_side_effects=True, vmem_limit_bytes=16 * 1024 * 1024
        ),
        name=f"spectral_{level}",
    )(pieces, weights)


def local(field, spectral, pointwise, bias):
    state = field[0]
    rows_here = state.shape[0]
    cols_here = state.shape[1]
    channels = state.shape[2]
    row_anchor = lax.axis_index("gx") * rows_here
    col_anchor = lax.axis_index("gy") * cols_here
    positions_x = row_anchor + jnp.arange(rows_here, dtype=jnp.int32)
    positions_y = col_anchor + jnp.arange(cols_here, dtype=jnp.int32)
    index_x = jnp.arange(KX, dtype=jnp.int32)
    freq_x = jnp.where(index_x < KX // 2, index_x, NX - KX + index_x)
    mem = lax.axis_size("mem")
    grid = lax.axis_size(("gx", "gy"))
    depth = KY // mem
    freq_y = jnp.arange(KY, dtype=jnp.int32).reshape(depth, mem).T.reshape(-1)
    angles_y = phase_angles(freq_y, positions_y, NY)
    cosine_y = jnp.cos(angles_y).T.astype(jnp.bfloat16)
    sine_y = jnp.sin(angles_y).T.astype(jnp.bfloat16)
    forward_y = jnp.concatenate(
        [jnp.concatenate([cosine_y, -sine_y], axis=1), jnp.concatenate([sine_y, cosine_y], axis=1)],
        axis=0,
    )
    doubling = jnp.where(freq_y == 0, 1.0, 2.0).astype(jnp.float32)[:, None]
    wcos = doubling * jnp.cos(angles_y)
    wsin = doubling * jnp.sin(angles_y)
    inverse_y = jnp.concatenate(
        [jnp.concatenate([wcos, wsin], axis=1), jnp.concatenate([-wsin, wcos], axis=1)], axis=0
    ).astype(jnp.bfloat16)
    scale_fwd = 1.0 / math.sqrt(NX * NY)
    scale_inv = 1.0 / math.sqrt(2 * KX * KY)
    own_rows = KX // grid
    weights = spectral.reshape(LAYERS, own_rows, 2, depth, channels, channels)

    def x_table():
        angles = phase_angles(freq_x, positions_x, NX)
        return (jnp.cos(angles).astype(jnp.bfloat16), jnp.sin(angles).astype(jnp.bfloat16))

    for level in range(LAYERS):
        current = state
        cosine_x, sine_x = x_table()
        table_x = jnp.concatenate([cosine_x, -sine_x], axis=0)
        partial_x = jnp.einsum(
            "kx,xyc->kyc", table_x, current, preferred_element_type=jnp.float32
        ).astype(jnp.bfloat16)
        joined = jnp.concatenate(
            [
                partial_x[: KX],
                partial_x[KX :],
            ],
            axis=1,
        )
        modes = jnp.einsum("kyc,yq->kqc", joined, forward_y, preferred_element_type=jnp.float32)
        pieces = (
            (modes * scale_fwd)
            .astype(jnp.bfloat16)
            .reshape(grid, own_rows, 2, mem, depth, mem, channels // mem)
            .transpose(5, 0, 2, 1, 4, 3, 6)
            .reshape(mem * grid, 2 * own_rows * depth, channels)
        )
        portion = spectral_mix(pieces, weights, level, own_rows, depth)
        flattened = (
            portion.reshape(grid, 2 * mem, own_rows, depth, channels)
            .transpose(0, 2, 1, 3, 4)
            .reshape(KX, 2 * KY, channels)
        )
        qmix = jnp.einsum(
            "kqc,qy->kyc", flattened, inverse_y, preferred_element_type=jnp.float32
        ).astype(jnp.bfloat16)
        stacked = jnp.concatenate([qmix[:, :cols_here], qmix[:, cols_here:]], axis=0)
        add_cosine_x, add_sine_x = x_table()
        add_table_x = jnp.concatenate([add_cosine_x, -add_sine_x], axis=0).T
        spatial = jnp.einsum(
            "xk,kyc->xyc", add_table_x, stacked, preferred_element_type=jnp.float32
        )
        linear = jnp.dot(
            current.reshape(rows_here * cols_here, channels),
            pointwise[level],
            preferred_element_type=jnp.float32,
        ).reshape(rows_here, cols_here, channels)
        mixed = spatial * scale_inv + linear + bias[level]
        state = jax.nn.gelu(mixed, approximate=False).astype(jnp.bfloat16)
    return state[None]


def solution(mesh):
    in_specs = (
        P("mem", "gx", "gy", None),
        P(None, ("gx", "gy"), None, None, "mem", None),
        P(),
        P(),
    )
    out_specs = P("mem", "gx", "gy", None)
    return jax.shard_map(local, mesh=mesh, in_specs=in_specs, out_specs=out_specs, check_vma=False)
```

```python
import functools
import math

import jax
import jax.numpy as jnp
from jax import lax
from jax.experimental import pallas as pl
from jax.experimental.pallas import tpu as pltpu
from jax.sharding import PartitionSpec as P

KX = 32
KY = 32
NX = 512
NY = 512
LAYERS = 3
MESH = pl.DeviceIdType.MESH


def phase_angles(frequency, position, period):
    product = frequency[:, None] * position[None, :] % period
    return 2.0 * math.pi / period * product.astype(jnp.float32)


def exchange(mem, n_gx, n_gy, shape, pieces_ref, weights_ref, out_ref, got, sums,
             partial, arrived, send_a, recv_a, send_b, recv_b, send_c, recv_c, own_sem):
    rows_j, depth = shape
    grid = n_gx * n_gy
    total = mem * grid
    m = lax.axis_index("mem")
    g = lax.axis_index("gx") * n_gy + lax.axis_index("gy")
    me = m * grid + g

    def place(mm, gg):
        return (mm, gg // n_gy, gg % n_gy)

    def place_all(d):
        return place(d // grid, d % grid)

    barrier = pltpu.get_barrier_semaphore()

    def greet(k, c):
        pl.semaphore_signal(
            barrier, inc=1, device_id=place_all((me + k) % total), device_id_type=MESH
        )
        return c

    lax.fori_loop(1, total, greet, 0)
    pl.semaphore_wait(barrier, total - 1)

    def copy_a(k, dst, slot):
        return pltpu.make_async_remote_copy(
            src_ref=pieces_ref.at[dst],
            dst_ref=got.at[slot],
            send_sem=send_a.at[k],
            recv_sem=recv_a.at[k],
            device_id=place_all(dst),
            device_id_type=MESH,
        )

    def start_a(k, c):
        copy_a(k, (me + k) % total, me).start()
        return c

    lax.fori_loop(1, total, start_a, 0)
    own = pltpu.make_async_copy(pieces_ref.at[me], got.at[me], own_sem)
    own.start()
    own.wait()

    def wait_a(k, c):
        copy_a(k, (me + k) % total, (me + total - k) % total).wait()
        return c

    lax.fori_loop(1, total, wait_a, 0)
    items = rows_j * depth
    for mm in range(mem):
        acc = got[mm * grid].astype(jnp.float32)
        for gg in range(1, grid):
            acc = acc + got[mm * grid + gg].astype(jnp.float32)
        for j in range(rows_j):
            for part in range(2):
                lo = (j * 2 + part) * depth
                sums[part * mem + mm, j * depth : (j + 1) * depth, :] = acc[lo : lo + depth]
    lanes = sums.shape[-1]
    wide = lanes // mem
    lane = lax.broadcasted_iota(jnp.int32, (2 * mem, lanes), 1)

    def mix(b, c):
        j = b // depth
        qq = b % depth
        x = sums[:, pl.ds(b, 1), :].reshape(2 * mem, lanes)
        parts = [
            jnp.where((lane >= h * wide) & (lane < (h + 1) * wide), x, 0.0) for h in range(mem)
        ]
        x = jnp.concatenate(parts, axis=0).astype(jnp.bfloat16)
        by_re = jnp.dot(x, weights_ref[j, 0, qq], preferred_element_type=jnp.float32)
        by_im = jnp.dot(x, weights_ref[j, 1, qq], preferred_element_type=jnp.float32)
        for h in range(mem):
            lo = h * 2 * mem
            re = by_re[lo : lo + mem] - by_im[lo + mem : lo + 2 * mem]
            im = by_im[lo : lo + mem] + by_re[lo + mem : lo + 2 * mem]
            for mm in range(mem):
                partial[mm, h, pl.ds(b, 1), :] = re[mm : mm + 1]
                partial[mm, mem + h, pl.ds(b, 1), :] = im[mm : mm + 1]
        return c

    lax.fori_loop(0, items, mix, 0, unroll=4)

    def copy_b(k, dst, slot):
        return pltpu.make_async_remote_copy(
            src_ref=partial.at[dst],
            dst_ref=arrived.at[slot],
            send_sem=send_b.at[k],
            recv_sem=recv_b.at[k],
            device_id=place(dst, g),
            device_id_type=MESH,
        )

    def start_b(k, c):
        copy_b(k, (m + k) % mem, k).start()
        return c

    lax.fori_loop(1, mem, start_b, 0)

    def wait_b(k, c):
        copy_b(k, (m + k) % mem, k).wait()
        return c

    lax.fori_loop(1, mem, wait_b, 0)
    block = partial[m]
    for k in range(1, mem):
        block = block + arrived[k]
    out_ref[g] = block.astype(out_ref.dtype)

    chips = grid // 2
    gx = lax.axis_index("gx")
    core = gx % 2
    chip = (gx // 2) * n_gy + lax.axis_index("gy")

    def spot(index, side):
        return ((index // n_gy) * 2 + side) * n_gy + index % n_gy

    def copy_c(k, slot):
        return pltpu.make_async_remote_copy(
            src_ref=out_ref.at[g],
            dst_ref=out_ref.at[slot],
            send_sem=send_c.at[k],
            recv_sem=recv_c.at[k],
            device_id=place(m, spot((chip + k) % chips, core)),
            device_id_type=MESH,
        )

    def forward(k, side):
        slot = spot((chip + chips - k) % chips, side)
        return pltpu.make_async_remote_copy(
            src_ref=out_ref.at[slot],
            dst_ref=out_ref.at[slot],
            send_sem=send_c.at[chips + k],
            recv_sem=recv_c.at[chips + k],
            device_id=place(m, spot(chip, 1 - core)),
            device_id_type=MESH,
        )

    def start_c(k, c):
        copy_c(k, g).start()
        return c

    lax.fori_loop(1, chips, start_c, 0)
    forward(0, core).start()

    def relay(k, c):
        copy_c(k, spot((chip + chips - k) % chips, core)).wait_recv()
        forward(k, core).start()
        return c

    lax.fori_loop(1, chips, relay, 0)

    def wait_c(k, c):
        copy_c(k, g).wait_send()
        return c

    lax.fori_loop(1, chips, wait_c, 0)

    def wait_f(k, c):
        forward(k, core).wait_send()
        forward(k, 1 - core).wait_recv()
        return c

    lax.fori_loop(0, chips, wait_f, 0)


def spectral_mix(pieces, weights, level, own_rows, depth):
    mem = lax.axis_size("mem")
    n_gx = lax.axis_size("gx")
    n_gy = lax.axis_size("gy")
    grid = n_gx * n_gy
    total = mem * grid
    channels = pieces.shape[-1]
    items = own_rows * depth
    dma = pltpu.SemaphoreType.DMA
    return pl.pallas_call(
        functools.partial(exchange, mem, n_gx, n_gy, (own_rows, depth)),
        out_shape=jax.ShapeDtypeStruct((grid, 2 * mem, items, channels), jnp.bfloat16),
        in_specs=[
            pl.BlockSpec(memory_space=pltpu.VMEM),
            pl.BlockSpec(memory_space=pltpu.VMEM),
        ],
        out_specs=pl.BlockSpec(memory_space=pltpu.VMEM),
        scratch_shapes=[
            pltpu.VMEM(pieces.shape, jnp.bfloat16),
            pltpu.VMEM((2 * mem, items, channels), jnp.float32),
            pltpu.VMEM((mem, 2 * mem, items, channels), jnp.float32),
            pltpu.VMEM((mem, 2 * mem, items, channels), jnp.float32),
            dma((total,)),
            dma((total,)),
            dma((mem,)),
            dma((mem,)),
            dma((grid,)),
            dma((grid,)),
            dma,
        ],
        compiler_params=pltpu.CompilerParams(
            collective_id=level, has_side_effects=True, vmem_limit_bytes=16 * 1024 * 1024
        ),
        name=f"spectral_{level}",
    )(pieces, weights)


def local(field, spectral, pointwise, bias):
    rows_here = field.shape[1]
    cols_here = field.shape[2]
    state = field[0]
    channels = state.shape[2]
    row_anchor = lax.axis_index("gx") * rows_here
    col_anchor = lax.axis_index("gy") * cols_here
    positions_x = row_anchor + jnp.arange(rows_here, dtype=jnp.int32)
    positions_y = col_anchor + jnp.arange(cols_here, dtype=jnp.int32)
    index_x = jnp.arange(KX, dtype=jnp.int32)
    freq_x = jnp.where(index_x < KX // 2, index_x, NX - KX + index_x)
    mem = lax.axis_size("mem")
    grid = lax.axis_size(("gx", "gy"))
    depth = KY // mem
    freq_y = jnp.arange(KY, dtype=jnp.int32).reshape(depth, mem).T.reshape(-1)
    angles_y = phase_angles(freq_y, positions_y, NY)
    cosine_y = jnp.cos(angles_y).T.astype(jnp.bfloat16)
    sine_y = jnp.sin(angles_y).T.astype(jnp.bfloat16)
    forward_y = jnp.concatenate(
        [jnp.concatenate([cosine_y, -sine_y], axis=1), jnp.concatenate([sine_y, cosine_y], axis=1)],
        axis=0,
    )
    doubling = jnp.where(freq_y == 0, 1.0, 2.0).astype(jnp.float32)[:, None]
    wcos = doubling * jnp.cos(angles_y)
    wsin = doubling * jnp.sin(angles_y)
    inverse_y = jnp.concatenate(
        [jnp.concatenate([wcos, wsin], axis=1), jnp.concatenate([-wsin, wcos], axis=1)], axis=0
    ).astype(jnp.bfloat16)
    scale_fwd = 1.0 / math.sqrt(NX * NY)
    scale_inv = 1.0 / math.sqrt(2 * KX * KY)
    own_rows = KX // grid
    weights = spectral.reshape(LAYERS, own_rows, 2, depth, channels, channels)

    def x_table():
        angles = phase_angles(freq_x, positions_x, NX)
        return (jnp.cos(angles).astype(jnp.bfloat16), jnp.sin(angles).astype(jnp.bfloat16))

    for level in range(LAYERS):
        current = state
        cosine_x, sine_x = x_table()
        table_x = jnp.concatenate([cosine_x, -sine_x], axis=0)
        partial_x = jnp.einsum(
            "kx,xyc->kyc", table_x, current, preferred_element_type=jnp.float32
        ).astype(jnp.bfloat16)
        joined = jnp.concatenate(
            [
                partial_x[: KX],
                partial_x[KX :],
            ],
            axis=1,
        )
        modes = jnp.einsum("kyc,yq->kqc", joined, forward_y, preferred_element_type=jnp.float32)
        rounded = (
            (modes * scale_fwd)
            .astype(jnp.bfloat16)
            .reshape(grid, own_rows * 2, mem, depth, channels)
        )
        wide = channels // mem
        pieces = jnp.stack(
            [
                jnp.concatenate(
                    [rounded[:, :, h, :, i * wide : (i + 1) * wide] for h in range(mem)], axis=-1
                )
                for i in range(mem)
            ]
        ).reshape(mem * grid, 2 * own_rows * depth, channels)
        portion = spectral_mix(pieces, weights[level], level, own_rows, depth)
        flattened = (
            portion.reshape(grid, 2 * mem, own_rows, depth, channels)
            .transpose(0, 2, 1, 3, 4)
            .reshape(KX, 2 * KY, channels)
        )
        qmix = jnp.einsum(
            "kqc,qy->kyc", flattened, inverse_y, preferred_element_type=jnp.float32
        ).astype(jnp.bfloat16)
        stacked = jnp.concatenate([qmix[:, :cols_here], qmix[:, cols_here:]], axis=0)
        add_cosine_x, add_sine_x = x_table()
        add_table_x = jnp.concatenate([add_cosine_x, -add_sine_x], axis=0).T
        spatial = jnp.einsum(
            "xk,kyc->xyc", add_table_x, stacked, preferred_element_type=jnp.float32
        )
        linear = jnp.dot(
            current.reshape(rows_here * cols_here, channels),
            pointwise[level],
            preferred_element_type=jnp.float32,
        ).reshape(rows_here, cols_here, channels)
        mixed = spatial * scale_inv + linear + bias[level]
        state = jax.nn.gelu(mixed, approximate=False).astype(jnp.bfloat16)
    return state[None]


def solution(mesh):
    in_specs = (
        P("mem", "gx", "gy", None),
        P(None, ("gx", "gy"), None, None, "mem", None),
        P(),
        P(),
    )
    out_specs = P("mem", "gx", "gy", None)
    return jax.shard_map(local, mesh=mesh, in_specs=in_specs, out_specs=out_specs, check_vma=False)
```

```python
import functools
import math

import jax
import jax.numpy as jnp
from jax import lax
from jax.experimental import pallas as pl
from jax.experimental.pallas import tpu as pltpu
from jax.sharding import PartitionSpec as P

KX = 32
KY = 32
NX = 512
NY = 512
LAYERS = 3
MESH = pl.DeviceIdType.MESH


def phase_angles(frequency, position, period):
    product = frequency[:, None] * position[None, :] % period
    return 2.0 * math.pi / period * product.astype(jnp.float32)


def exchange(mem, n_gx, n_gy, shape, pieces_ref, weights_ref, out_ref, near, staged, got, sums,
             partial, arrived, send_p, recv_p, send_a, recv_a, send_b, recv_b, send_c, recv_c, own_sem):
    rows_j, depth = shape
    grid = n_gx * n_gy
    total = mem * grid
    m = lax.axis_index("mem")
    g = lax.axis_index("gx") * n_gy + lax.axis_index("gy")

    def place(mm, gg):
        return (mm, gg // n_gy, gg % n_gy)

    chips = grid // 2
    half = total // 2
    pairs = n_gx // 2
    gx = lax.axis_index("gx")
    core = gx % 2
    chip = (gx // 2) * n_gy + lax.axis_index("gy")
    here = m * chips + chip

    def spot(index, side):
        return ((index // n_gy) * 2 + side) * n_gy + index % n_gy

    def place_chip(d):
        return place(d // chips, spot(d % chips, core))

    partner = place(m, spot(chip, 1 - core))
    barrier = pltpu.get_barrier_semaphore()

    def greet(k, c):
        pl.semaphore_signal(
            barrier, inc=1, device_id=place_chip((here + k) % half), device_id_type=MESH
        )
        return c

    pl.semaphore_signal(barrier, inc=1, device_id=partner, device_id_type=MESH)
    lax.fori_loop(1, half, greet, 0)
    pl.semaphore_wait(barrier, half)

    def run(t, side):
        return pl.ds((t // pairs) * grid + ((t % pairs) * 2 + side) * n_gy, n_gy)

    def copy_p(t):
        return pltpu.make_async_remote_copy(
            src_ref=pieces_ref.at[run(t, 1 - core)],
            dst_ref=near.at[pl.ds(t * n_gy, n_gy)],
            send_sem=send_p.at[t],
            recv_sem=recv_p.at[t],
            device_id=partner,
            device_id_type=MESH,
        )

    def start_p(t, c):
        copy_p(t).start()
        return c

    lax.fori_loop(0, mem * pairs, start_p, 0)

    def add_p(t, c):
        copy_p(t).wait()
        rows = pl.ds(t * n_gy, n_gy)
        both = pieces_ref[run(t, core)].astype(jnp.float32) + near[rows].astype(jnp.float32)
        staged[rows] = both.astype(jnp.bfloat16)
        return c

    lax.fori_loop(0, mem * pairs, add_p, 0)

    def copy_a(k, dst, slot):
        return pltpu.make_async_remote_copy(
            src_ref=staged.at[dst],
            dst_ref=got.at[slot],
            send_sem=send_a.at[k],
            recv_sem=recv_a.at[k],
            device_id=place_chip(dst),
            device_id_type=MESH,
        )

    def start_a(k, c):
        copy_a(k, (here + k) % half, here).start()
        return c

    lax.fori_loop(1, half, start_a, 0)
    own = pltpu.make_async_copy(staged.at[here], got.at[here], own_sem)
    own.start()
    own.wait()

    def wait_a(k, c):
        copy_a(k, (here + k) % half, (here + half - k) % half).wait()
        return c

    lax.fori_loop(1, half, wait_a, 0)
    items = rows_j * depth
    for mm in range(mem):
        acc = got[mm * chips].astype(jnp.float32)
        for gg in range(1, chips):
            acc = acc + got[mm * chips + gg].astype(jnp.float32)
        for j in range(rows_j):
            for part in range(2):
                lo = (j * 2 + part) * depth
                sums[part * mem + mm, j * depth : (j + 1) * depth, :] = acc[lo : lo + depth]
    lanes = sums.shape[-1]
    wide = lanes // mem
    lane = lax.broadcasted_iota(jnp.int32, (2 * mem, lanes), 1)

    def mix(b, c):
        j = b // depth
        qq = b % depth
        x = sums[:, pl.ds(b, 1), :].reshape(2 * mem, lanes)
        parts = [
            jnp.where((lane >= h * wide) & (lane < (h + 1) * wide), x, 0.0) for h in range(mem)
        ]
        x = jnp.concatenate(parts, axis=0).astype(jnp.bfloat16)
        by_re = jnp.dot(x, weights_ref[j, 0, qq], preferred_element_type=jnp.float32)
        by_im = jnp.dot(x, weights_ref[j, 1, qq], preferred_element_type=jnp.float32)
        for h in range(mem):
            lo = h * 2 * mem
            re = by_re[lo : lo + mem] - by_im[lo + mem : lo + 2 * mem]
            im = by_im[lo : lo + mem] + by_re[lo + mem : lo + 2 * mem]
            for mm in range(mem):
                partial[mm, h, pl.ds(b, 1), :] = re[mm : mm + 1]
                partial[mm, mem + h, pl.ds(b, 1), :] = im[mm : mm + 1]
        return c

    lax.fori_loop(0, items, mix, 0, unroll=8)

    def copy_b(k, dst, slot):
        return pltpu.make_async_remote_copy(
            src_ref=partial.at[dst],
            dst_ref=arrived.at[slot],
            send_sem=send_b.at[k],
            recv_sem=recv_b.at[k],
            device_id=place(dst, g),
            device_id_type=MESH,
        )

    def start_b(k, c):
        copy_b(k, (m + k) % mem, k).start()
        return c

    lax.fori_loop(1, mem, start_b, 0)

    def wait_b(k, c):
        copy_b(k, (m + k) % mem, k).wait()
        return c

    lax.fori_loop(1, mem, wait_b, 0)
    block = partial[m]
    for k in range(1, mem):
        block = block + arrived[k]
    out_ref[g] = block.astype(out_ref.dtype)

    def copy_c(k, slot):
        return pltpu.make_async_remote_copy(
            src_ref=out_ref.at[g],
            dst_ref=out_ref.at[slot],
            send_sem=send_c.at[k],
            recv_sem=recv_c.at[k],
            device_id=place(m, spot((chip + k) % chips, core)),
            device_id_type=MESH,
        )

    def forward(k, side):
        slot = spot((chip + chips - k) % chips, side)
        return pltpu.make_async_remote_copy(
            src_ref=out_ref.at[slot],
            dst_ref=out_ref.at[slot],
            send_sem=send_c.at[chips + k],
            recv_sem=recv_c.at[chips + k],
            device_id=place(m, spot(chip, 1 - core)),
            device_id_type=MESH,
        )

    def start_c(k, c):
        copy_c(k, g).start()
        return c

    lax.fori_loop(1, chips, start_c, 0)
    forward(0, core).start()

    def relay(k, c):
        copy_c(k, spot((chip + chips - k) % chips, core)).wait_recv()
        forward(k, core).start()
        return c

    lax.fori_loop(1, chips, relay, 0)

    def wait_c(k, c):
        copy_c(k, g).wait_send()
        return c

    lax.fori_loop(1, chips, wait_c, 0)

    def wait_f(k, c):
        forward(k, core).wait_send()
        forward(k, 1 - core).wait_recv()
        return c

    lax.fori_loop(0, chips, wait_f, 0)


def spectral_mix(pieces, weights, level, own_rows, depth):
    mem = lax.axis_size("mem")
    n_gx = lax.axis_size("gx")
    n_gy = lax.axis_size("gy")
    grid = n_gx * n_gy
    total = mem * grid
    channels = pieces.shape[-1]
    items = own_rows * depth
    dma = pltpu.SemaphoreType.DMA
    return pl.pallas_call(
        functools.partial(exchange, mem, n_gx, n_gy, (own_rows, depth)),
        out_shape=jax.ShapeDtypeStruct((grid, 2 * mem, items, channels), jnp.bfloat16),
        in_specs=[
            pl.BlockSpec(memory_space=pltpu.VMEM),
            pl.BlockSpec(memory_space=pltpu.VMEM),
        ],
        out_specs=pl.BlockSpec(memory_space=pltpu.VMEM),
        scratch_shapes=[
            pltpu.VMEM((total // 2,) + pieces.shape[1:], jnp.bfloat16),
            pltpu.VMEM((total // 2,) + pieces.shape[1:], jnp.bfloat16),
            pltpu.VMEM((total // 2,) + pieces.shape[1:], jnp.bfloat16),
            pltpu.VMEM((2 * mem, items, channels), jnp.float32),
            pltpu.VMEM((mem, 2 * mem, items, channels), jnp.float32),
            pltpu.VMEM((mem, 2 * mem, items, channels), jnp.float32),
            dma((mem * n_gx // 2,)),
            dma((mem * n_gx // 2,)),
            dma((total // 2,)),
            dma((total // 2,)),
            dma((mem,)),
            dma((mem,)),
            dma((grid,)),
            dma((grid,)),
            dma,
        ],
        compiler_params=pltpu.CompilerParams(
            collective_id=level, has_side_effects=True, vmem_limit_bytes=16 * 1024 * 1024
        ),
        name=f"spectral_{level}",
    )(pieces, weights)


def local(field, spectral, pointwise, bias):
    rows_here = field.shape[1]
    cols_here = field.shape[2]
    state = field[0]
    channels = state.shape[2]
    row_anchor = lax.axis_index("gx") * rows_here
    col_anchor = lax.axis_index("gy") * cols_here
    positions_x = row_anchor + jnp.arange(rows_here, dtype=jnp.int32)
    positions_y = col_anchor + jnp.arange(cols_here, dtype=jnp.int32)
    index_x = jnp.arange(KX, dtype=jnp.int32)
    freq_x = jnp.where(index_x < KX // 2, index_x, NX - KX + index_x)
    mem = lax.axis_size("mem")
    grid = lax.axis_size(("gx", "gy"))
    depth = KY // mem
    freq_y = jnp.arange(KY, dtype=jnp.int32).reshape(depth, mem).T.reshape(-1)
    angles_y = phase_angles(freq_y, positions_y, NY)
    cosine_y = jnp.cos(angles_y).T.astype(jnp.bfloat16)
    sine_y = jnp.sin(angles_y).T.astype(jnp.bfloat16)
    forward_y = jnp.concatenate(
        [jnp.concatenate([cosine_y, -sine_y], axis=1), jnp.concatenate([sine_y, cosine_y], axis=1)],
        axis=0,
    )
    doubling = jnp.where(freq_y == 0, 1.0, 2.0).astype(jnp.float32)[:, None]
    wcos = doubling * jnp.cos(angles_y)
    wsin = doubling * jnp.sin(angles_y)
    inverse_y = jnp.concatenate(
        [jnp.concatenate([wcos, wsin], axis=1), jnp.concatenate([-wsin, wcos], axis=1)], axis=0
    ).astype(jnp.bfloat16)
    scale_fwd = 1.0 / math.sqrt(NX * NY)
    scale_inv = 1.0 / math.sqrt(2 * KX * KY)
    own_rows = KX // grid
    weights = spectral.reshape(LAYERS, own_rows, 2, depth, channels, channels)

    def x_table():
        angles = phase_angles(freq_x, positions_x, NX)
        return (jnp.cos(angles).astype(jnp.bfloat16), jnp.sin(angles).astype(jnp.bfloat16))

    for level in range(LAYERS):
        current = state
        cosine_x, sine_x = x_table()
        table_x = jnp.concatenate([cosine_x, -sine_x], axis=0)
        partial_x = jnp.einsum(
            "kx,xyc->kyc", table_x, current, preferred_element_type=jnp.float32
        ).astype(jnp.bfloat16)
        joined = jnp.concatenate(
            [
                partial_x[: KX],
                partial_x[KX :],
            ],
            axis=1,
        )
        modes = jnp.einsum("kyc,yq->kqc", joined, forward_y, preferred_element_type=jnp.float32)
        rounded = (
            (modes * scale_fwd)
            .astype(jnp.bfloat16)
            .reshape(grid, own_rows * 2, mem, depth, channels)
        )
        wide = channels // mem
        pieces = jnp.stack(
            [
                jnp.concatenate(
                    [rounded[:, :, h, :, i * wide : (i + 1) * wide] for h in range(mem)], axis=-1
                )
                for i in range(mem)
            ]
        ).reshape(mem * grid, 2 * own_rows * depth, channels)
        portion = spectral_mix(pieces, weights[level], level, own_rows, depth)
        flattened = (
            portion.reshape(grid, 2 * mem, own_rows, depth, channels)
            .transpose(0, 2, 1, 3, 4)
            .reshape(KX, 2 * KY, channels)
        )
        qmix = jnp.einsum(
            "kqc,qy->kyc", flattened, inverse_y, preferred_element_type=jnp.float32
        ).astype(jnp.bfloat16)
        stacked = jnp.concatenate([qmix[:, :cols_here], qmix[:, cols_here:]], axis=0)
        add_cosine_x, add_sine_x = x_table()
        add_table_x = jnp.concatenate([add_cosine_x, -add_sine_x], axis=0).T
        spatial = jnp.einsum(
            "xk,kyc->xyc", add_table_x, stacked, preferred_element_type=jnp.float32
        )
        linear = jnp.dot(
            current.reshape(rows_here * cols_here, channels),
            pointwise[level],
            preferred_element_type=jnp.float32,
        ).reshape(rows_here, cols_here, channels)
        mixed = spatial * scale_inv + linear + bias[level]
        state = jax.nn.gelu(mixed, approximate=False).astype(jnp.bfloat16)
    return state[None]


def solution(mesh):
    in_specs = (
        P("mem", "gx", "gy", None),
        P(None, ("gx", "gy"), None, None, "mem", None),
        P(),
        P(),
    )
    out_specs = P("mem", "gx", "gy", None)
    return jax.shard_map(local, mesh=mesh, in_specs=in_specs, out_specs=out_specs, check_vma=False)
```
